512 devices in a mesh: row: 8 (over x, core), col: 16 (over z), depth: 4 (over y).
Axes of the slice: x: 4, y: 4, z: 16, core: 2. Of those that a mesh axis runs over, the one named last changes fastest.
Arguments:
- k_parts: bfloat16 [2, 4096, 4096], P(None, 'row', 'col'), as said below
- p_parts: bfloat16 [2, 4096, 4096], P(None, 'row', 'col'), as said below
- k_mask: int32 [64, 64], P('row', 'col'), may hold values from 0 to 1, as said below
- p_mask: int32 [64, 64], P('row', 'col'), may hold values from 0 to 1, as said below
- atoms: int32 [64], replicated, may hold values from 0 to 15, as said below
- classes: int32 [16, 16], replicated, may hold values from 0 to 3
- rates: float32 [4], replicated, may hold values from 0.5 to 8
Outputs:
- derivative: float32 [2, 4096, 4096], P(None, ('row', 'depth'), 'col')
The draws below stay inside these ranges and needn't reach their ends.
Inputs may be any that keep to these rules, and one draw needn't show every extreme that they name: k_parts[0] is symmetric and k_parts[1] antisymmetric, so the Kohn-Sham matrix is Hermitian. p_parts[0] is symmetric and p_parts[1] antisymmetric, so the density matrix is Hermitian. `k_mask`: symmetric; every diagonal tile is kept; each tile row keeps a band of tiles around the diagonal of its own half-width, from 0 to 16 tiles, besides scattered tiles further away. `p_mask`: symmetric; every diagonal tile is kept; each tile row keeps a band of tiles around the diagonal of its own half-width, from 0 to 16 tiles, besides scattered tiles further away. `atoms`: never falling along the tiles; every atom block holds at least one tile.
All inputs are finite; a program needn't handle non-finite values.
Results may differ from the reference program's by a relative error of at most 0.0003.
Values may be sent and summed in bfloat16 or wider, within the bound.
A program may use at most 64 MiB of HBM per device.

```python
import math
import jax
import jax.numpy as jnp

TILE = 64
NCLASS = 4
N = 4096
NT = 64
NA = 16


def hermitian_pair(key):
    first = jax.random.normal(jax.random.fold_in(key, 1), (N, N), jnp.float32)
    second = jax.random.normal(jax.random.fold_in(key, 2), (N, N), jnp.float32)
    scale = (2.0 * TILE) ** (-0.5)
    real_part = (first + first.T) * scale
    imag_part = (second - second.T) * scale
    return jnp.stack((real_part, imag_part)).astype(jnp.bfloat16)


def band_mask(key):
    widths = jax.random.randint(jax.random.fold_in(key, 1), (NT,), 0, NT // 4 + 1)
    distant = jax.random.randint(jax.random.fold_in(key, 2), (NT, NT), 0, 8) == 0
    places = jnp.arange(NT, dtype=jnp.int32)
    spacing = jnp.abs(places[:, None] - places[None, :])
    reach = jnp.maximum(widths[:, None], widths[None, :])
    keep = (spacing <= reach) | distant | distant.T
    return keep.astype(jnp.int32)


def draw_k_parts(key, part):
    return hermitian_pair(jax.random.fold_in(key, 11))


def draw_p_parts(key, part):
    return hermitian_pair(jax.random.fold_in(key, 12))


def draw_k_mask(key, part):
    return band_mask(jax.random.fold_in(key, 21))


def draw_p_mask(key, part):
    return band_mask(jax.random.fold_in(key, 22))


def draw_atoms(key, part):
    candidates = jnp.arange(1, NT, dtype=jnp.int32)
    shuffled = jax.random.permutation(jax.random.fold_in(key, 31), candidates)
    bounds = shuffled[:NA - 1]
    places = jnp.arange(NT, dtype=jnp.int32)
    return jnp.sum((bounds[None, :] <= places[:, None]).astype(jnp.int32), axis=1).astype(jnp.int32)


def set_ends(result, key, least, top_value):
    longest = result.shape.index(max(result.shape))
    spots = []
    for shift in (0, 1):
        where = [jax.random.randint(jax.random.fold_in(key, axis), (), 0, length) for axis, length in enumerate(result.shape)]
        where[longest] = (where[longest] + shift) % result.shape[longest]
        spots.append(tuple(where))
    return result.at[spots[0]].set(least).at[spots[1]].set(top_value)


def setup_inputs(seed: int = 0) -> dict:
    splits = jax.random.split(jax.random.key(seed), 8)
    return {
        "k_parts": draw_k_parts(jax.random.fold_in(splits[7], 71), 0),
        "p_parts": draw_p_parts(jax.random.fold_in(splits[7], 71), 0),
        "k_mask": draw_k_mask(jax.random.fold_in(splits[7], 71), 0),
        "p_mask": draw_p_mask(jax.random.fold_in(splits[7], 71), 0),
        "atoms": draw_atoms(jax.random.fold_in(splits[7], 71), 0),
        "classes": set_ends(jax.random.randint(splits[5], (NA, NA), 0, NCLASS), jax.random.fold_in(splits[5], 1), 0, NCLASS - 1).astype(jnp.int32),
        "rates": jnp.clip(jnp.exp(jax.random.uniform(splits[6], (NCLASS,), jnp.float32, math.log(0.5), math.log(8.0))), 0.5, 8.0),
    }


def expand_tiles(mask):
    return jnp.repeat(jnp.repeat(mask, TILE, 0), TILE, 1).astype(jnp.bfloat16)


def product(left, right):
    return jnp.dot(left, right, preferred_element_type=jnp.float32)


def reference(k_parts, p_parts, k_mask, p_mask, atoms, classes, rates):
    k_full = k_parts * expand_tiles(k_mask)[None]
    p_full = p_parts * expand_tiles(p_mask)[None]
    k_real, k_imag = k_full[0], k_full[1]
    p_real, p_imag = p_full[0], p_full[1]
    z_real = product(k_real, p_real) - product(k_imag, p_imag) - product(p_real, k_real) + product(p_imag, k_imag)
    z_imag = product(k_real, p_imag) + product(k_imag, p_real) - product(p_real, k_imag) - product(p_imag, k_real)
    atom_rows = jnp.repeat(atoms, TILE)
    kinds = classes[atom_rows[:, None], atom_rows[None, :]]
    differ = (atom_rows[:, None] != atom_rows[None, :]).astype(rates.dtype)
    gamma = rates[kinds] * differ
    p_float = p_full.astype(rates.dtype)
    return jnp.stack((z_imag - gamma * p_float[0], -z_real - gamma * p_float[1]))
```

```python
import functools

import jax
import jax.numpy as jnp
from jax import lax
from jax.experimental import pallas as pl
from jax.experimental.pallas import tpu as pltpu
from jax.sharding import PartitionSpec as P

TILE = 64
MESH = pl.DeviceIdType.MESH


def expand_mask(mask, tile, dtype):
    rows_t, cols_t = mask.shape
    grid = jnp.broadcast_to(mask[:, None, :, None], (rows_t, tile, cols_t, tile))
    return grid.reshape(rows_t * tile, cols_t * tile).astype(dtype)


def rcopy(src, dst, send_sem, recv_sem, device):
    return pltpu.make_async_remote_copy(
        src_ref=src,
        dst_ref=dst,
        send_sem=send_sem,
        recv_sem=recv_sem,
        device_id=device,
        device_id_type=MESH,
    )


def kernel(
    nr, nz, nd,
    k_ref, p_ref, atoms_ref, classes_ref, rates_ref,
    out_ref,
    cols, rows, acc, zs, zr, xs, xr, ds, dr, ls,
):
    r = lax.axis_index("row")
    z = lax.axis_index("col")
    d = lax.axis_index("depth")
    x = r // 2
    q = r % 2
    nx = nr // 2
    rows_here, cols_here = k_ref.shape[1], k_ref.shape[2]
    rows_out = rows_here // nd
    per_row = rows_here // cols_here
    half = nz // 2
    own_rows = pl.ds(pl.multiple_of(d * rows_out, rows_out), rows_out)

    def rx(step):
        return 2 * lax.rem(x + (step + nx), nx) + q

    def zz(step):
        return lax.rem(z + (step + nz), nz)

    up_z, down_z = (r, zz(1), d), (r, zz(-1), d)
    up_x, down_x = (rx(1), z, d), (rx(-1), z, d)
    twin = (2 * x + 1 - q, z, d)
    z_to = (up_z, down_z)
    x_to = (up_x, down_x)

    barrier = pltpu.get_barrier_semaphore()
    for peer in (up_z, down_z, up_x, down_x, twin):
        pl.semaphore_signal(barrier, inc=1, device_id=peer, device_id_type=MESH)
    pl.semaphore_wait(barrier, 5)

    own = (k_ref, p_ref)

    def row_part(block, part):
        return rows.at[block, pl.ds(2 * part, 2)]

    def col_part(block, part):
        return cols.at[block, pl.ds(2 * (1 - part), 2)]

    def z_copy(way, dist, part):
        block = zz(1 - dist) if way == 0 else zz(dist - 1)
        src = own[part].at[:, own_rows, :] if dist == 1 else row_part(block, part)
        return rcopy(
            src, row_part(block, part), zs.at[way, dist - 1, part],
            zr.at[way, dist - 1, part], z_to[way],
        )

    def z_arrival(way, dist, part):
        block = zz(-dist) if way == 0 else zz(dist)
        slot = row_part(block, part)
        return rcopy(
            slot, slot, zs.at[way, dist - 1, part], zr.at[way, dist - 1, part], z_to[way]
        )

    def z_has(way, dist, part):
        return dist < half or (dist == half and part == way)

    def x_copy(way, idx):
        part = way if idx != 1 else 1 - way
        block = rx(0) if idx < 2 else (rx(-1) if way == 0 else rx(1))
        src = own[part] if idx < 2 else col_part(block, part)
        return rcopy(src, col_part(block, part), xs.at[way, idx], xr.at[way, idx], x_to[way])

    def x_arrival(way, idx):
        part = way if idx != 1 else 1 - way
        step = 1 if idx < 2 else 2
        block = rx(-step) if way == 0 else rx(step)
        slot = col_part(block, part)
        return rcopy(slot, slot, xs.at[way, idx], xr.at[way, idx], x_to[way]), block, part

    def twin_copy(sem, block, part, local):
        src = own[part] if local else col_part(block, part)
        return rcopy(src, col_part(block, part), ds.at[sem], dr.at[sem], twin)

    def twin_arrival(sem, block, part):
        other = block + 1 - 2 * q
        slot = col_part(other, part)
        return rcopy(slot, slot, ds.at[sem], dr.at[sem], twin)

    sent = []
    twins = []

    def start(copy):
        copy.start()
        sent.append(copy)

    for part in (0, 1):
        for way in (0, 1):
            start(z_copy(way, 1, part))
    for idx in (0, 1):
        for way in (0, 1):
            start(x_copy(way, idx))
    for part in (0, 1):
        start(twin_copy(part, r, part, True))
        twins.append((part, r, part))
    local = []
    for part in (0, 1):
        local.append(pltpu.make_async_copy(own[part], col_part(r, part), ls.at[part]))
        local.append(
            pltpu.make_async_copy(
                own[part].at[:, own_rows, :], row_part(z, part), ls.at[2 + part]
            )
        )
    for copy in local:
        copy.start()
    acc[...] = jnp.zeros_like(acc)
    for copy in local:
        copy.wait()

    def x_event(idx):
        for way in (0, 1):
            copy, block, part = x_arrival(way, idx)
            copy.wait_recv()
            if idx == 0:
                start(x_copy(way, 2))
            sem = 2 + 2 * idx + way
            start(twin_copy(sem, block, part, False))
            twins.append((sem, block, part))

    def twin_waits():
        for sem, block, part in twins:
            twin_arrival(sem, block, part).wait_recv()
        twins.clear()

    def multiply(block):
        row = rows[block]
        kre, kim, pre, pim = row[0], row[1], row[2], row[3]
        left = jnp.concatenate(
            (
                jnp.concatenate((kre, -kim, -pre, pim), axis=1),
                jnp.concatenate((kim, kre, -pim, -pre), axis=1),
            ),
            axis=0,
        )
        start_row = pl.multiple_of(lax.rem(block, per_row) * cols_here, cols_here)
        right = cols[block // per_row, :, pl.ds(start_row, cols_here), :]
        right = right.reshape(4 * cols_here, cols_here)
        acc[...] += jnp.dot(left, right, preferred_element_type=jnp.float32)

    far = lax.rem(x + nx // 2, nx)

    def is_far(block):
        return block // (per_row * 2) == far

    def near_blocks(first, last):
        def step(o, carry):
            block = lax.rem(z + (nz + first) + o, nz)

            @pl.when(jnp.logical_not(is_far(block)))
            def _():
                multiply(block)

            return carry

        lax.fori_loop(0, last + 1 - first, step, 0)

    for dist in range(1, half):
        for part in (0, 1):
            for way in (0, 1):
                z_arrival(way, dist, part).wait_recv()
                if z_has(way, dist + 1, part):
                    start(z_copy(way, dist + 1, part))
            if dist == half - 2 and part == 0:
                near_blocks(-(half - 3), -2)
            if dist == half - 2 and part == 1:
                near_blocks(-1, 1)
            if dist == half - 1 and part == 0:
                near_blocks(2, half - 3)
        if dist == half - 5:
            x_event(0)
        if dist == half - 3:
            x_event(1)
            twin_waits()
    x_event(2)
    near_blocks(half - 2, half - 1)
    near_blocks(-(half - 1), -(half - 2))
    twin_waits()

    def far_step(o, carry):
        block = lax.rem(z + (half + 1) + o, nz)

        @pl.when(is_far(block))
        def _():
            multiply(block)

        return carry

    lax.fori_loop(0, nz - 1, far_step, 0)
    for way in (0, 1):
        z_arrival(way, half, way).wait_recv()
    multiply(zz(half))

    lane = lax.broadcasted_iota(jnp.int32, (1, cols_here), 1) // TILE
    for i in range(rows_out // TILE):
        atom_row = atoms_ref[(r * rows_here + d * rows_out) // TILE + i]
        gamma = jnp.zeros((1, cols_here), jnp.float32)
        for j in range(cols_here // TILE):
            atom_col = atoms_ref[z * (cols_here // TILE) + j]
            rate = rates_ref[classes_ref[atom_row, atom_col]]
            rate = jnp.where(atom_row != atom_col, rate, 0.0)
            gamma = jnp.where(lane == j, rate, gamma)
        here = pl.ds(pl.multiple_of(d * rows_out + i * TILE, TILE), TILE)
        p_re = p_ref[0, here, :].astype(jnp.float32)
        p_im = p_ref[1, here, :].astype(jnp.float32)
        z_re = acc[pl.ds(i * TILE, TILE), :]
        z_im = acc[pl.ds(rows_out + i * TILE, TILE), :]
        out_ref[0, pl.ds(i * TILE, TILE), :] = z_im - gamma * p_re
        out_ref[1, pl.ds(i * TILE, TILE), :] = -z_re - gamma * p_im

    for copy in sent:
        copy.wait_send()


def solution(mesh):
    nr, nz, nd = mesh.shape["row"], mesh.shape["col"], mesh.shape["depth"]

    def body(k_parts, p_parts, k_mask, p_mask, atoms, classes, rates):
        k_local = k_parts * expand_mask(k_mask, TILE, jnp.bfloat16)[None]
        p_local = p_parts * expand_mask(p_mask, TILE, jnp.bfloat16)[None]
        rows_here, cols_here = k_local.shape[1:]
        rows_out = rows_here // nd
        half = nz // 2
        return pl.pallas_call(
            functools.partial(kernel, nr, nz, nd),
            out_shape=jax.ShapeDtypeStruct((2, rows_out, cols_here), jnp.float32),
            in_specs=[pl.BlockSpec(memory_space=pltpu.VMEM)] * 2
            + [pl.BlockSpec(memory_space=pltpu.SMEM)] * 3,
            out_specs=pl.BlockSpec(memory_space=pltpu.VMEM),
            scratch_shapes=[
                pltpu.VMEM((nr, 4, rows_here, cols_here), jnp.bfloat16),
                pltpu.VMEM((nz, 4, rows_out, cols_here), jnp.bfloat16),
                pltpu.VMEM((2 * rows_out, cols_here), jnp.float32),
                pltpu.SemaphoreType.DMA((2, half, 2)),
                pltpu.SemaphoreType.DMA((2, half, 2)),
                pltpu.SemaphoreType.DMA((2, 3)),
                pltpu.SemaphoreType.DMA((2, 3)),
                pltpu.SemaphoreType.DMA((8,)),
                pltpu.SemaphoreType.DMA((8,)),
                pltpu.SemaphoreType.DMA((4,)),
            ],
            compiler_params=pltpu.CompilerParams(
                collective_id=0, has_side_effects=True, vmem_limit_bytes=40 * 2**20
            ),
        )(k_local, p_local, atoms, classes, rates)

    return jax.shard_map(
        body,
        mesh=mesh,
        in_specs=(
            P(None, "row", "col"),
            P(None, "row", "col"),
            P("row", "col"),
            P("row", "col"),
            P(),
            P(),
            P(),
        ),
        out_specs=P(None, ("row", "depth"), "col"),
        check_vma=False,
    )
```

```python
import functools

import jax
import jax.numpy as jnp
from jax import lax
from jax.experimental import pallas as pl
from jax.experimental.pallas import tpu as pltpu
from jax.sharding import PartitionSpec as P

TILE = 64
CHUNKS = 4
MESH = pl.DeviceIdType.MESH


def rcopy(src, dst, send_sem, recv_sem, device):
    return pltpu.make_async_remote_copy(
        src_ref=src,
        dst_ref=dst,
        send_sem=send_sem,
        recv_sem=recv_sem,
        device_id=device,
        device_id_type=MESH,
    )


def kernel(
    nr, nz, nd,
    k_hbm, p_hbm, k_mask_hbm, p_mask_hbm, atoms_hbm, classes_hbm, rates_hbm,
    out_ref,
    k_ref, p_ref, k_mask_ref, p_mask_ref, atoms_ref, classes_ref, rates_ref,
    cols, rows, acc, zs, zr, xs, xr, ds, dr, ls, fs,
):
    fetches = [
        pltpu.make_async_copy(src, dst, fs.at[i])
        for i, (src, dst) in enumerate(
            (
                (k_mask_hbm, k_mask_ref),
                (k_hbm, k_ref),
                (p_mask_hbm, p_mask_ref),
                (p_hbm, p_ref),
                (atoms_hbm, atoms_ref),
                (classes_hbm, classes_ref),
                (rates_hbm, rates_ref),
            )
        )
    ]
    for copy in fetches:
        copy.start()
    r = lax.axis_index("row")
    z = lax.axis_index("col")
    d = lax.axis_index("depth")
    x = r // 2
    q = r % 2
    nx = nr // 2
    rows_here, cols_here = k_ref.shape[1], k_ref.shape[2]
    rows_out = rows_here // nd
    per_row = rows_here // cols_here
    half = nz // 2
    own_rows = pl.ds(pl.multiple_of(d * rows_out, rows_out), rows_out)

    def rx(step):
        return 2 * lax.rem(x + (step + nx), nx) + q

    def zz(step):
        return lax.rem(z + (step + nz), nz)

    up_z, down_z = (r, zz(1), d), (r, zz(-1), d)
    up_x, down_x = (rx(1), z, d), (rx(-1), z, d)
    twin = (2 * x + 1 - q, z, d)
    z_to = (up_z, down_z)
    x_to = (up_x, down_x)

    barrier = pltpu.get_barrier_semaphore()
    for peer in (up_z, down_z, up_x, down_x, twin):
        pl.semaphore_signal(barrier, inc=1, device_id=peer, device_id_type=MESH)

    for copy in fetches:
        copy.wait()
    lane = lax.broadcasted_iota(jnp.int32, (1, cols_here), 1) // TILE
    for raw, mask_ref, comp in ((k_ref, k_mask_ref, 2), (p_ref, p_mask_ref, 0)):
        for i in range(rows_here // TILE):
            keep = jnp.zeros((1, cols_here), jnp.float32)
            for j in range(cols_here // TILE):
                keep = jnp.where(lane == j, mask_ref[j, i].astype(jnp.float32), keep)
            keep = keep.astype(jnp.bfloat16)
            tile = pl.ds(i * TILE, TILE)
            for c in (0, 1):
                cols[r, comp + c, tile, :] = raw[c, tile, :] * keep

    gammas = []
    for i in range(rows_out // TILE):
        atom_row = atoms_ref[(r * rows_here + d * rows_out) // TILE + i]
        gamma = jnp.zeros((1, cols_here), jnp.float32)
        for j in range(cols_here // TILE):
            atom_col = atoms_ref[z * (cols_here // TILE) + j]
            rate = rates_ref[classes_ref[atom_row, atom_col]]
            rate = jnp.where(atom_row != atom_col, rate, 0.0)
            gamma = jnp.where(lane == j, rate, gamma)
        gammas.append(gamma)
    acc[...] = jnp.zeros_like(acc)

    pl.semaphore_wait(barrier, 5)
    own = (cols.at[r, pl.ds(2, 2)], cols.at[r, pl.ds(0, 2)])

    piece = 2 * rows_out // CHUNKS

    def row_part(block, part):
        return rows.at[block, pl.ds(2 * (part % 2), 2), pl.ds(part // 2 * piece, piece)]

    def own_part(part):
        first = pl.multiple_of(d * rows_out + part // 2 * piece, piece)
        return own[part % 2].at[:, pl.ds(first, piece), :]

    def col_part(block, part):
        return cols.at[block, pl.ds(2 * (1 - part), 2)]

    def z_copy(way, dist, part):
        block = zz(1 - dist) if way == 0 else zz(dist - 1)
        src = own_part(part) if dist == 1 else row_part(block, part)
        return rcopy(
            src, row_part(block, part), zs.at[way, dist - 1, part],
            zr.at[way, dist - 1, part], z_to[way],
        )

    def z_arrival(way, dist, part):
        block = zz(-dist) if way == 0 else zz(dist)
        slot = row_part(block, part)
        return rcopy(
            slot, slot, zs.at[way, dist - 1, part], zr.at[way, dist - 1, part], z_to[way]
        )

    def z_has(way, dist, part):
        return dist < half or (dist == half and part % 2 == way)

    def x_copy(way, idx):
        part = way if idx != 1 else 1 - way
        block = rx(0) if idx < 2 else (rx(-1) if way == 0 else rx(1))
        src = own[part] if idx < 2 else col_part(block, part)
        return rcopy(src, col_part(block, part), xs.at[way, idx], xr.at[way, idx], x_to[way])

    def x_arrival(way, idx):
        part = way if idx != 1 else 1 - way
        step = 1 if idx < 2 else 2
        block = rx(-step) if way == 0 else rx(step)
        slot = col_part(block, part)
        return rcopy(slot, slot, xs.at[way, idx], xr.at[way, idx], x_to[way]), block, part

    def twin_copy(sem, block, part, local):
        src = own[part] if local else col_part(block, part)
        return rcopy(src, col_part(block, part), ds.at[sem], dr.at[sem], twin)

    def twin_arrival(sem, block, part):
        other = block + 1 - 2 * q
        slot = col_part(other, part)
        return rcopy(slot, slot, ds.at[sem], dr.at[sem], twin)

    sent = []
    twins = []

    def start(copy):
        copy.start()
        sent.append(copy)

    for part in range(CHUNKS):
        for way in (0, 1):
            start(z_copy(way, 1, part))
    for idx in (0, 1):
        for way in (0, 1):
            start(x_copy(way, idx))
    for part in (0, 1):
        start(twin_copy(part, r, part, True))
        twins.append((part, r, part))
    local = []
    for part in (0, 1):
        local.append(
            pltpu.make_async_copy(
                own[part].at[:, own_rows, :], rows.at[z, pl.ds(2 * part, 2)], ls.at[part]
            )
        )
    for copy in local:
        copy.start()
    for copy in local:
        copy.wait()

    def x_event(idx):
        for way in (0, 1):
            copy, block, part = x_arrival(way, idx)
            copy.wait_recv()
            if idx == 0:
                start(x_copy(way, 2))
            sem = 2 + 2 * idx + way
            start(twin_copy(sem, block, part, False))
            twins.append((sem, block, part))

    def twin_waits():
        for sem, block, part in twins:
            twin_arrival(sem, block, part).wait_recv()
        twins.clear()

    def multiply(block):
        row = rows[block]
        kre, kim, pre, pim = row[0], row[1], row[2], row[3]
        left = jnp.concatenate(
            (
                jnp.concatenate((kre, -kim, -pre, pim), axis=1),
                jnp.concatenate((kim, kre, -pim, -pre), axis=1),
            ),
            axis=0,
        )
        start_row = pl.multiple_of(lax.rem(block, per_row) * cols_here, cols_here)
        right = cols[block // per_row, :, pl.ds(start_row, cols_here), :]
        right = right.reshape(4 * cols_here, cols_here)
        acc[...] += jnp.dot(left, right, preferred_element_type=jnp.float32)

    far = lax.rem(x + nx // 2, nx)

    def is_far(block):
        return block // (per_row * 2) == far

    def near_blocks(first, last):
        def step(o, carry):
            block = lax.rem(z + (nz + first) + o, nz)

            @pl.when(jnp.logical_not(is_far(block)))
            def _():
                multiply(block)

            return carry

        lax.fori_loop(0, last + 1 - first, step, 0)

    for dist in range(1, half):
        for part in range(CHUNKS):
            for way in (0, 1):
                z_arrival(way, dist, part).wait_recv()
                if z_has(way, dist + 1, part):
                    start(z_copy(way, dist + 1, part))
            if dist == half - 2 and part == CHUNKS // 2 - 1:
                near_blocks(-(half - 3), -2)
            if dist == half - 2 and part == CHUNKS - 1:
                near_blocks(-1, 1)
            if dist == half - 1 and part == CHUNKS // 2 - 1:
                near_blocks(2, half - 3)
        if dist == half - 5:
            x_event(0)
        if dist == half - 3:
            x_event(1)
            twin_waits()
    x_event(2)
    near_blocks(half - 2, half - 1)
    near_blocks(-(half - 1), -(half - 2))
    twin_waits()

    def far_step(o, carry):
        block = lax.rem(z + (half + 1) + o, nz)

        @pl.when(is_far(block))
        def _():
            multiply(block)

        return carry

    lax.fori_loop(0, nz - 1, far_step, 0)
    for part in range(CHUNKS):
        z_arrival(part % 2, half, part).wait_recv()
    multiply(zz(half))

    for i in range(rows_out // TILE):
        tile = pl.ds(i * TILE, TILE)
        p_re = rows[z, 2, tile, :].astype(jnp.float32)
        p_im = rows[z, 3, tile, :].astype(jnp.float32)
        z_re = acc[tile, :]
        z_im = acc[pl.ds(rows_out + i * TILE, TILE), :]
        out_ref[0, tile, :] = z_im - gammas[i] * p_re
        out_ref[1, tile, :] = -z_re - gammas[i] * p_im

    for copy in sent:
        copy.wait_send()


def solution(mesh):
    nr, nz, nd = mesh.shape["row"], mesh.shape["col"], mesh.shape["depth"]

    def body(k_parts, p_parts, k_mask, p_mask, atoms, classes, rates):
        rows_here, cols_here = k_parts.shape[1:]
        rows_out = rows_here // nd
        half = nz // 2
        return pl.pallas_call(
            functools.partial(kernel, nr, nz, nd),
            out_shape=jax.ShapeDtypeStruct((2, rows_out, cols_here), jnp.float32),
            in_specs=[pl.BlockSpec(memory_space=pltpu.HBM)] * 7,
            out_specs=pl.BlockSpec(memory_space=pltpu.VMEM),
            scratch_shapes=[
                pltpu.VMEM(k_parts.shape, k_parts.dtype),
                pltpu.VMEM(p_parts.shape, p_parts.dtype),
                pltpu.SMEM(k_mask.T.shape, k_mask.dtype),
                pltpu.SMEM(p_mask.T.shape, p_mask.dtype),
                pltpu.SMEM(atoms.shape, atoms.dtype),
                pltpu.SMEM(classes.shape, classes.dtype),
                pltpu.SMEM(rates.shape, rates.dtype),
                pltpu.VMEM((nr, 4, rows_here, cols_here), jnp.bfloat16),
                pltpu.VMEM((nz, 4, rows_out, cols_here), jnp.bfloat16),
                pltpu.VMEM((2 * rows_out, cols_here), jnp.float32),
                pltpu.SemaphoreType.DMA((2, half, CHUNKS)),
                pltpu.SemaphoreType.DMA((2, half, CHUNKS)),
                pltpu.SemaphoreType.DMA((2, 3)),
                pltpu.SemaphoreType.DMA((2, 3)),
                pltpu.SemaphoreType.DMA((8,)),
                pltpu.SemaphoreType.DMA((8,)),
                pltpu.SemaphoreType.DMA((2,)),
                pltpu.SemaphoreType.DMA((7,)),
            ],
            compiler_params=pltpu.CompilerParams(
                collective_id=0, has_side_effects=True, vmem_limit_bytes=67_043_328
            ),
        )(k_parts, p_parts, k_mask.T, p_mask.T, atoms, classes, rates)

    return jax.shard_map(
        body,
        mesh=mesh,
        in_specs=(
            P(None, "row", "col"),
            P(None, "row", "col"),
            P("row", "col"),
            P("row", "col"),
            P(),
            P(),
            P(),
        ),
        out_specs=P(None, ("row", "depth"), "col"),
        check_vma=False,
    )
```

```python
import functools

import jax
import jax.numpy as jnp
from jax import lax
from jax.experimental import pallas as pl
from jax.experimental.pallas import tpu as pltpu
from jax.sharding import PartitionSpec as P

TILE = 64
CHUNKS = 4
MESH = pl.DeviceIdType.MESH


def rcopy(src, dst, send_sem, recv_sem, device):
    return pltpu.make_async_remote_copy(
        src_ref=src,
        dst_ref=dst,
        send_sem=send_sem,
        recv_sem=recv_sem,
        device_id=device,
        device_id_type=MESH,
    )


def kernel(
    nr, nz, nd,
    k_hbm, p_hbm, k_mask_hbm, p_mask_hbm, atoms_hbm, classes_hbm, rates_hbm,
    out_ref,
    k_ref, p_ref, k_mask_ref, p_mask_ref, atoms_ref, classes_ref, rates_ref,
    cols, rows, acc, zs, zr, xs, xr, ys, yr, ds, dr, ls, fs,
):
    fetches = [
        pltpu.make_async_copy(src, dst, fs.at[i])
        for i, (src, dst) in enumerate(
            (
                (k_mask_hbm, k_mask_ref),
                (k_hbm, k_ref),
                (p_mask_hbm, p_mask_ref),
                (p_hbm, p_ref),
                (atoms_hbm, atoms_ref),
                (classes_hbm, classes_ref),
                (rates_hbm, rates_ref),
            )
        )
    ]
    for copy in fetches:
        copy.start()
    r = lax.axis_index("row")
    z = lax.axis_index("col")
    d = lax.axis_index("depth")
    x = r // 2
    q = r % 2
    nx = nr // 2
    rows_here, cols_here = k_ref.shape[1], k_ref.shape[2]
    rows_out = rows_here // nd
    per_row = rows_here // cols_here
    half = nz // 2
    own_rows = pl.ds(pl.multiple_of(d * rows_out, rows_out), rows_out)

    def rx(step):
        return 2 * lax.rem(x + (step + nx), nx) + q

    def zz(step):
        return lax.rem(z + (step + nz), nz)

    up_z, down_z = (r, zz(1), d), (r, zz(-1), d)
    up_x, down_x = (rx(1), z, d), (rx(-1), z, d)
    twin = (2 * x + 1 - q, z, d)
    z_to = (up_z, down_z)
    x_to = (up_x, down_x)
    up_y, down_y = (r, z, lax.rem(d + 1, nd)), (r, z, lax.rem(d + nd - 1, nd))
    y_to = (up_y, down_y)

    barrier = pltpu.get_barrier_semaphore()
    for peer in (up_z, down_z, up_x, down_x, up_y, down_y, twin):
        pl.semaphore_signal(barrier, inc=1, device_id=peer, device_id_type=MESH)

    for copy in fetches:
        copy.wait()
    lane = lax.broadcasted_iota(jnp.int32, (1, cols_here), 1) // TILE
    for raw, mask_ref, comp in ((k_ref, k_mask_ref, 2), (p_ref, p_mask_ref, 0)):
        for i in range(rows_here // TILE):
            keep = jnp.zeros((1, cols_here), jnp.float32)
            for j in range(cols_here // TILE):
                keep = jnp.where(lane == j, mask_ref[j, i].astype(jnp.float32), keep)
            keep = keep.astype(jnp.bfloat16)
            tile = pl.ds(i * TILE, TILE)
            for c in (0, 1):
                cols[r, comp + c, tile, :] = raw[c, tile, :] * keep

    gammas = []
    for i in range(rows_out // TILE):
        atom_row = atoms_ref[(r * rows_here + d * rows_out) // TILE + i]
        gamma = jnp.zeros((1, cols_here), jnp.float32)
        for j in range(cols_here // TILE):
            atom_col = atoms_ref[z * (cols_here // TILE) + j]
            rate = rates_ref[classes_ref[atom_row, atom_col]]
            rate = jnp.where(atom_row != atom_col, rate, 0.0)
            gamma = jnp.where(lane == j, rate, gamma)
        gammas.append(gamma)
    acc[...] = jnp.zeros_like(acc)

    pl.semaphore_wait(barrier, 7)
    own = (cols.at[r, pl.ds(2, 2)], cols.at[r, pl.ds(0, 2)])

    piece = 2 * rows_out // CHUNKS

    def row_part(block, part):
        return rows.at[block, pl.ds(2 * (part % 2), 2), pl.ds(part // 2 * piece, piece)]

    def own_part(part):
        first = pl.multiple_of(d * rows_out + part // 2 * piece, piece)
        return own[part % 2].at[:, pl.ds(first, piece), :]

    def col_part(block, part):
        return cols.at[block, pl.ds(2 * (1 - part), 2)]

    def z_copy(way, dist, part):
        block = zz(1 - dist) if way == 0 else zz(dist - 1)
        src = own_part(part) if dist == 1 else row_part(block, part)
        return rcopy(
            src, row_part(block, part), zs.at[way, dist - 1, part],
            zr.at[way, dist - 1, part], z_to[way],
        )

    def z_arrival(way, dist, part):
        block = zz(-dist) if way == 0 else zz(dist)
        slot = row_part(block, part)
        return rcopy(
            slot, slot, zs.at[way, dist - 1, part], zr.at[way, dist - 1, part], z_to[way]
        )

    def z_has(way, dist, part):
        return dist < half or (dist == half and part % 2 == way)

    def quarter(block, turn):
        first = lax.rem(d + (turn + nd), nd) * rows_out
        return cols.at[block, :, pl.ds(pl.multiple_of(first, rows_out), rows_out), :]

    def x_turn(way, idx):
        return (0, nd // 2)[way if idx == 2 else idx]

    def x_copy(way, idx):
        step = 0 if idx < 2 else 1
        slot = quarter(rx(-step) if way == 0 else rx(step), x_turn(way, idx))
        return rcopy(slot, slot, xs.at[way, idx], xr.at[way, idx], x_to[way])

    def x_arrival(way, idx):
        step = 1 if idx < 2 else 2
        block = rx(-step) if way == 0 else rx(step)
        slot = quarter(block, x_turn(way, idx))
        return rcopy(slot, slot, xs.at[way, idx], xr.at[way, idx], x_to[way]), block

    y_blocks = (rx(-1), rx(1), rx(-2))

    def y_copy(way, j):
        slot = quarter(y_blocks[j], 0)
        return rcopy(slot, slot, ys.at[way, j], yr.at[way, j], y_to[way])

    def y_arrival(way, j):
        slot = quarter(y_blocks[j], -1 if way == 0 else 1)
        return rcopy(slot, slot, ys.at[way, j], yr.at[way, j], y_to[way])

    def to_twin(sem, block, turn):
        slot = quarter(block, turn)
        start(rcopy(slot, slot, ds.at[sem], dr.at[sem], twin))
        twins.append((sem, block, turn))

    def own_to_twin(part, block):
        slot = col_part(block, part)
        return rcopy(slot, slot, ds.at[part], dr.at[part], twin)

    sent = []
    twins = []

    def start(copy):
        copy.start()
        sent.append(copy)

    for part in range(CHUNKS):
        for way in (0, 1):
            start(z_copy(way, 1, part))
    for idx in (0, 1):
        for way in (0, 1):
            start(x_copy(way, idx))
    for part in (0, 1):
        start(own_to_twin(part, r))
    local = []
    for part in (0, 1):
        local.append(
            pltpu.make_async_copy(
                own[part].at[:, own_rows, :], rows.at[z, pl.ds(2 * part, 2)], ls.at[part]
            )
        )
    for copy in local:
        copy.start()
    for copy in local:
        copy.wait()

    def x_event(idx):
        for way in (0, 1):
            copy, block = x_arrival(way, idx)
            copy.wait_recv()
            if idx < 2 and idx == way:
                start(x_copy(way, 2))
            if x_turn(way, idx) == 0:
                j = 2 if idx == 2 else way
                for y_way in (0, 1):
                    start(y_copy(y_way, j))
            to_twin(2 + 2 * idx + way, block, x_turn(way, idx))

    def y_event(j):
        for way in (0, 1):
            y_arrival(way, j).wait_recv()
            to_twin(8 + 2 * j + way, y_blocks[j], -1 if way == 0 else 1)

    def twin_waits():
        for part in (0, 1):
            own_to_twin(part, r + 1 - 2 * q).wait_recv()
        for sem, block, turn in twins:
            slot = quarter(block + 1 - 2 * q, turn)
            rcopy(slot, slot, ds.at[sem], dr.at[sem], twin).wait_recv()

    def multiply(block):
        row = rows[block]
        kre, kim, pre, pim = row[0], row[1], row[2], row[3]
        left = jnp.concatenate(
            (
                jnp.concatenate((kre, -kim, -pre, pim), axis=1),
                jnp.concatenate((kim, kre, -pim, -pre), axis=1),
            ),
            axis=0,
        )
        start_row = pl.multiple_of(lax.rem(block, per_row) * cols_here, cols_here)
        right = cols[block // per_row, :, pl.ds(start_row, cols_here), :]
        right = right.reshape(4 * cols_here, cols_here)
        acc[...] += jnp.dot(left, right, preferred_element_type=jnp.float32)

    def blocks(first, last):
        def step(o, carry):
            multiply(lax.rem(z + (nz + first) + o, nz))
            return carry

        lax.fori_loop(0, last + 1 - first, step, 0)

    events = {
        (2, 0): lambda: x_event(0),
        (3, 0): lambda: x_event(1),
        (4, 0): lambda: x_event(2),
        (4, 2): lambda: (y_event(0), y_event(1)),
        (5, 3): lambda: y_event(2),
        (6, 0): twin_waits,
        (6, 1): lambda: blocks(-5, -4),
        (6, 2): lambda: blocks(-3, -2),
        (6, 3): lambda: blocks(-1, 1),
        (7, 0): lambda: blocks(2, 3),
        (7, 1): lambda: blocks(4, 5),
    }
    for dist in range(1, half):
        for part in range(CHUNKS):
            for way in (0, 1):
                z_arrival(way, dist, part).wait_recv()
                if z_has(way, dist + 1, part):
                    start(z_copy(way, dist + 1, part))
            events.get((dist, part), lambda: None)()
    blocks(6, 7)
    blocks(-7, -6)
    for part in range(CHUNKS):
        z_arrival(part % 2, half, part).wait_recv()
    multiply(zz(half))

    for i in range(rows_out // TILE):
        tile = pl.ds(i * TILE, TILE)
        p_re = rows[z, 2, tile, :].astype(jnp.float32)
        p_im = rows[z, 3, tile, :].astype(jnp.float32)
        z_re = acc[tile, :]
        z_im = acc[pl.ds(rows_out + i * TILE, TILE), :]
        out_ref[0, tile, :] = z_im - gammas[i] * p_re
        out_ref[1, tile, :] = -z_re - gammas[i] * p_im

    for copy in sent:
        copy.wait_send()


def solution(mesh):
    nr, nz, nd = mesh.shape["row"], mesh.shape["col"], mesh.shape["depth"]

    def body(k_parts, p_parts, k_mask, p_mask, atoms, classes, rates):
        rows_here, cols_here = k_parts.shape[1:]
        rows_out = rows_here // nd
        half = nz // 2
        return pl.pallas_call(
            functools.partial(kernel, nr, nz, nd),
            out_shape=jax.ShapeDtypeStruct((2, rows_out, cols_here), jnp.float32),
            in_specs=[pl.BlockSpec(memory_space=pltpu.HBM)] * 7,
            out_specs=pl.BlockSpec(memory_space=pltpu.VMEM),
            scratch_shapes=[
                pltpu.VMEM(k_parts.shape, k_parts.dtype),
                pltpu.VMEM(p_parts.shape, p_parts.dtype),
                pltpu.SMEM(k_mask.T.shape, k_mask.dtype),
                pltpu.SMEM(p_mask.T.shape, p_mask.dtype),
                pltpu.SMEM(atoms.shape, atoms.dtype),
                pltpu.SMEM(classes.shape, classes.dtype),
                pltpu.SMEM(rates.shape, rates.dtype),
                pltpu.VMEM((nr, 4, rows_here, cols_here), jnp.bfloat16),
                pltpu.VMEM((nz, 4, rows_out, cols_here), jnp.bfloat16),
                pltpu.VMEM((2 * rows_out, cols_here), jnp.float32),
                pltpu.SemaphoreType.DMA((2, half, CHUNKS)),
                pltpu.SemaphoreType.DMA((2, half, CHUNKS)),
                pltpu.SemaphoreType.DMA((2, 3)),
                pltpu.SemaphoreType.DMA((2, 3)),
                pltpu.SemaphoreType.DMA((2, 3)),
                pltpu.SemaphoreType.DMA((2, 3)),
                pltpu.SemaphoreType.DMA((14,)),
                pltpu.SemaphoreType.DMA((14,)),
                pltpu.SemaphoreType.DMA((2,)),
                pltpu.SemaphoreType.DMA((7,)),
            ],
            compiler_params=pltpu.CompilerParams(
                collective_id=0, has_side_effects=True, vmem_limit_bytes=67_043_328
            ),
        )(k_parts, p_parts, k_mask.T, p_mask.T, atoms, classes, rates)

    return jax.shard_map(
        body,
        mesh=mesh,
        in_specs=(
            P(None, "row", "col"),
            P(None, "row", "col"),
            P("row", "col"),
            P("row", "col"),
            P(),
            P(),
            P(),
        ),
        out_specs=P(None, ("row", "depth"), "col"),
        check_vma=False,
    )
```

```python
import functools

import jax
import jax.numpy as jnp
from jax import lax
from jax.experimental import pallas as pl
from jax.experimental.pallas import tpu as pltpu
from jax.sharding import PartitionSpec as P

TILE = 64
CHUNKS = 4
MESH = pl.DeviceIdType.MESH


def rcopy(src, dst, send_sem, recv_sem, device):
    return pltpu.make_async_remote_copy(
        src_ref=src,
        dst_ref=dst,
        send_sem=send_sem,
        recv_sem=recv_sem,
        device_id=device,
        device_id_type=MESH,
    )


def kernel(
    nr, nz, nd,
    k_hbm, p_hbm, k_mask_hbm, p_mask_hbm, atoms_hbm, classes_hbm, rates_hbm,
    out_ref,
    k_ref, p_ref, k_mask_ref, p_mask_ref, atoms_ref, classes_ref, rates_ref,
    cols, rows, acc, zs, zr, xs, xr, ys, yr, ds, dr, ls, fs,
):
    fetches = [
        pltpu.make_async_copy(src, dst, fs.at[i])
        for i, (src, dst) in enumerate(
            (
                (k_mask_hbm, k_mask_ref),
                (k_hbm, k_ref),
                (p_mask_hbm, p_mask_ref),
                (p_hbm, p_ref),
                (atoms_hbm, atoms_ref),
                (classes_hbm, classes_ref),
                (rates_hbm, rates_ref),
            )
        )
    ]
    for copy in fetches:
        copy.start()
    r = lax.axis_index("row")
    z = lax.axis_index("col")
    d = lax.axis_index("depth")
    x = r // 2
    q = r % 2
    nx = nr // 2
    rows_here, cols_here = k_ref.shape[1], k_ref.shape[2]
    rows_out = rows_here // nd
    per_row = rows_here // cols_here
    half = nz // 2
    own_rows = pl.ds(pl.multiple_of(d * rows_out, rows_out), rows_out)

    def rx(step):
        return 2 * lax.rem(x + (step + nx), nx) + q

    def zz(step):
        return lax.rem(z + (step + nz), nz)

    up_z, down_z = (r, zz(1), d), (r, zz(-1), d)
    up_x, down_x = (rx(1), z, d), (rx(-1), z, d)
    twin = (2 * x + 1 - q, z, d)
    z_to = (up_z, down_z)
    x_to = (up_x, down_x)
    up_y, down_y = (r, z, lax.rem(d + 1, nd)), (r, z, lax.rem(d + nd - 1, nd))
    y_to = (up_y, down_y)

    barrier = pltpu.get_barrier_semaphore()
    for peer in (up_z, down_z, up_x, down_x, up_y, down_y, twin):
        pl.semaphore_signal(barrier, inc=1, device_id=peer, device_id_type=MESH)

    for copy in fetches:
        copy.wait()
    lane = lax.broadcasted_iota(jnp.int32, (1, cols_here), 1) // TILE
    for raw, mask_ref, comp in ((k_ref, k_mask_ref, 2), (p_ref, p_mask_ref, 0)):
        for i in range(rows_here // TILE):
            keep = jnp.zeros((1, cols_here), jnp.float32)
            for j in range(cols_here // TILE):
                keep = jnp.where(lane == j, mask_ref[j, i].astype(jnp.float32), keep)
            keep = keep.astype(jnp.bfloat16)
            tile = pl.ds(i * TILE, TILE)
            for c in (0, 1):
                cols[r, comp + c, tile, :] = raw[c, tile, :] * keep

    gammas = []
    for i in range(rows_out // TILE):
        atom_row = atoms_ref[(r * rows_here + d * rows_out) // TILE + i]
        gamma = jnp.zeros((1, cols_here), jnp.float32)
        for j in range(cols_here // TILE):
            atom_col = atoms_ref[z * (cols_here // TILE) + j]
            rate = rates_ref[classes_ref[atom_row, atom_col]]
            rate = jnp.where(atom_row != atom_col, rate, 0.0)
            gamma = jnp.where(lane == j, rate, gamma)
        gammas.append(gamma)
    acc[...] = jnp.zeros_like(acc)

    pl.semaphore_wait(barrier, 7)
    own = (cols.at[r, pl.ds(2, 2)], cols.at[r, pl.ds(0, 2)])

    piece = 2 * rows_out // CHUNKS

    def row_part(block, part):
        return rows.at[block, pl.ds(2 * (part % 2), 2), pl.ds(part // 2 * piece, piece)]

    def own_part(part):
        first = pl.multiple_of(d * rows_out + part // 2 * piece, piece)
        return own[part % 2].at[:, pl.ds(first, piece), :]

    def col_part(block, part):
        return cols.at[block, pl.ds(2 * (1 - part), 2)]

    def z_copy(way, dist, part):
        block = zz(1 - dist) if way == 0 else zz(dist - 1)
        src = own_part(part) if dist == 1 else row_part(block, part)
        return rcopy(
            src, row_part(block, part), zs.at[way, dist - 1, part],
            zr.at[way, dist - 1, part], z_to[way],
        )

    def z_arrival(way, dist, part):
        block = zz(-dist) if way == 0 else zz(dist)
        slot = row_part(block, part)
        return rcopy(
            slot, slot, zs.at[way, dist - 1, part], zr.at[way, dist - 1, part], z_to[way]
        )

    def z_has(way, dist, part):
        return dist < half or (dist == half and part % 2 == way)

    def quarter(block, turn):
        first = lax.rem(d + (turn + nd), nd) * rows_out
        return cols.at[block, :, pl.ds(pl.multiple_of(first, rows_out), rows_out), :]

    def x_turn(way, idx):
        return (0, nd // 2)[way if idx == 2 else idx]

    def x_copy(way, idx):
        step = 0 if idx < 2 else 1
        slot = quarter(rx(-step) if way == 0 else rx(step), x_turn(way, idx))
        return rcopy(slot, slot, xs.at[way, idx], xr.at[way, idx], x_to[way])

    def x_arrival(way, idx):
        step = 1 if idx < 2 else 2
        block = rx(-step) if way == 0 else rx(step)
        slot = quarter(block, x_turn(way, idx))
        return rcopy(slot, slot, xs.at[way, idx], xr.at[way, idx], x_to[way]), block

    y_blocks = (rx(-1), rx(1), rx(-2))

    def y_copy(way, j):
        slot = quarter(y_blocks[j], 0)
        return rcopy(slot, slot, ys.at[way, j], yr.at[way, j], y_to[way])

    def y_arrival(way, j):
        slot = quarter(y_blocks[j], -1 if way == 0 else 1)
        return rcopy(slot, slot, ys.at[way, j], yr.at[way, j], y_to[way])

    def to_twin(sem, block, turn):
        slot = quarter(block, turn)
        start(rcopy(slot, slot, ds.at[sem], dr.at[sem], twin))
        twins.append((sem, block, turn))

    def own_to_twin(part, block):
        slot = col_part(block, part)
        return rcopy(slot, slot, ds.at[part], dr.at[part], twin)

    sent = []
    twins = []

    def start(copy):
        copy.start()
        sent.append(copy)

    for part in range(CHUNKS):
        for way in (0, 1):
            start(z_copy(way, 1, part))
    for idx in (0, 1):
        for way in (0, 1):
            start(x_copy(way, idx))
    for part in (0, 1):
        start(own_to_twin(part, r))
    local = []
    for part in (0, 1):
        local.append(
            pltpu.make_async_copy(
                own[part].at[:, own_rows, :], rows.at[z, pl.ds(2 * part, 2)], ls.at[part]
            )
        )
    for copy in local:
        copy.start()
    for copy in local:
        copy.wait()

    def x_event(idx):
        for way in (0, 1):
            copy, block = x_arrival(way, idx)
            copy.wait_recv()
            if idx < 2 and idx == way:
                start(x_copy(way, 2))
            if x_turn(way, idx) == 0:
                j = 2 if idx == 2 else way
                for y_way in (0, 1):
                    start(y_copy(y_way, j))
            to_twin(2 + 2 * idx + way, block, x_turn(way, idx))

    def y_event(j):
        for way in (0, 1):
            y_arrival(way, j).wait_recv()
            to_twin(8 + 2 * j + way, y_blocks[j], -1 if way == 0 else 1)

    def twin_waits():
        for part in (0, 1):
            own_to_twin(part, r + 1 - 2 * q).wait_recv()
        for sem, block, turn in twins:
            slot = quarter(block + 1 - 2 * q, turn)
            rcopy(slot, slot, ds.at[sem], dr.at[sem], twin).wait_recv()

    def multiply(block):
        row = rows[block]
        kre, kim, pre, pim = row[0], row[1], row[2], row[3]
        left = jnp.concatenate(
            (
                jnp.concatenate((kre, -kim, -pre, pim), axis=1),
                jnp.concatenate((kim, kre, -pim, -pre), axis=1),
            ),
            axis=0,
        )
        start_row = pl.multiple_of(lax.rem(block, per_row) * cols_here, cols_here)
        right = cols[block // per_row, :, pl.ds(start_row, cols_here), :]
        right = right.reshape(4 * cols_here, cols_here)
        acc[...] += jnp.dot(left, right, preferred_element_type=jnp.float32)

    def blocks(first, last):
        def step(o, carry):
            multiply(lax.rem(z + (nz + first) + o, nz))
            return carry

        lax.fori_loop(0, last + 1 - first, step, 0)

    events = {
        (2, 0): lambda: x_event(0),
        (3, 0): lambda: x_event(1),
        (4, 0): lambda: x_event(2),
        (4, 2): lambda: (y_event(0), y_event(1)),
        (5, 3): lambda: y_event(2),
        (6, 0): twin_waits,
        (6, 1): lambda: blocks(-5, -4),
        (6, 2): lambda: blocks(-3, -2),
        (6, 3): lambda: blocks(-1, 1),
        (7, 0): lambda: blocks(2, 3),
        (7, 1): lambda: blocks(4, 5),
    }
    for dist in range(1, half):
        for part in range(CHUNKS):
            for way in (0, 1):
                z_arrival(way, dist, part).wait_recv()
                if z_has(way, dist + 1, part):
                    start(z_copy(way, dist + 1, part))
            events.get((dist, part), lambda: None)()
    blocks(6, 7)
    blocks(-7, -6)
    for part in range(CHUNKS):
        z_arrival(part % 2, half, part).wait_recv()
    multiply(zz(half))

    for i in range(rows_out // TILE):
        tile = pl.ds(i * TILE, TILE)
        p_re = rows[z, 2, tile, :].astype(jnp.float32)
        p_im = rows[z, 3, tile, :].astype(jnp.float32)
        z_re = acc[tile, :]
        z_im = acc[pl.ds(rows_out + i * TILE, TILE), :]
        out_ref[0, tile, :] = z_im - gammas[i] * p_re
        out_ref[1, tile, :] = -z_re - gammas[i] * p_im

    for copy in sent:
        copy.wait_send()


def solution(mesh):
    nr, nz, nd = mesh.shape["row"], mesh.shape["col"], mesh.shape["depth"]

    def body(k_parts, p_parts, k_mask, p_mask, atoms, classes, rates):
        rows_here, cols_here = k_parts.shape[1:]
        rows_out = rows_here // nd
        half = nz // 2
        return pl.pallas_call(
            functools.partial(kernel, nr, nz, nd),
            out_shape=jax.ShapeDtypeStruct((2, rows_out, cols_here), jnp.float32),
            in_specs=[pl.BlockSpec(memory_space=pltpu.HBM)] * 7,
            out_specs=pl.BlockSpec(memory_space=pltpu.VMEM),
            scratch_shapes=[
                pltpu.VMEM(k_parts.shape, k_parts.dtype),
                pltpu.VMEM(p_parts.shape, p_parts.dtype),
                pltpu.SMEM(k_mask.T.shape, k_mask.dtype),
                pltpu.SMEM(p_mask.T.shape, p_mask.dtype),
                pltpu.SMEM(atoms.shape, atoms.dtype),
                pltpu.SMEM(classes.shape, classes.dtype),
                pltpu.SMEM(rates.shape, rates.dtype),
                pltpu.VMEM((nr, 4, rows_here, cols_here), jnp.bfloat16),
                pltpu.VMEM((nz, 4, rows_out, cols_here), jnp.bfloat16),
                pltpu.VMEM((2 * rows_out, cols_here), jnp.float32),
                pltpu.SemaphoreType.DMA((2, half, CHUNKS)),
                pltpu.SemaphoreType.DMA((2, half, CHUNKS)),
                pltpu.SemaphoreType.DMA((2, 3)),
                pltpu.SemaphoreType.DMA((2, 3)),
                pltpu.SemaphoreType.DMA((2, 3)),
                pltpu.SemaphoreType.DMA((2, 3)),
                pltpu.SemaphoreType.DMA((14,)),
                pltpu.SemaphoreType.DMA((14,)),
                pltpu.SemaphoreType.DMA((2,)),
                pltpu.SemaphoreType.DMA((7,)),
            ],
            compiler_params=pltpu.CompilerParams(
                collective_id=0, has_side_effects=True, vmem_limit_bytes=40 * 2**20
            ),
        )(*(pltpu.with_memory_space_constraint(v, pltpu.HBM) for v in (k_parts, p_parts, k_mask.T, p_mask.T, atoms, classes, rates)))

    return jax.shard_map(
        body,
        mesh=mesh,
        in_specs=(
            P(None, "row", "col"),
            P(None, "row", "col"),
            P("row", "col"),
            P("row", "col"),
            P(),
            P(),
            P(),
        ),
        out_specs=P(None, ("row", "depth"), "col"),
        check_vma=False,
    )
```

```python
import functools

import jax
import jax.numpy as jnp
from jax import lax
from jax.experimental import pallas as pl
from jax.experimental.pallas import tpu as pltpu
from jax.sharding import PartitionSpec as P

TILE = 64
CHUNKS = 4
MESH = pl.DeviceIdType.MESH


def rcopy(src, dst, send_sem, recv_sem, device):
    return pltpu.make_async_remote_copy(
        src_ref=src,
        dst_ref=dst,
        send_sem=send_sem,
        recv_sem=recv_sem,
        device_id=device,
        device_id_type=MESH,
    )


def kernel(
    nr, nz, nd,
    k_hbm, p_hbm, k_mask_hbm, p_mask_hbm, atoms_hbm, classes_hbm, rates_hbm,
    out_ref,
    k_ref, p_ref, k_mask_ref, p_mask_ref, atoms_ref, classes_ref, rates_ref,
    cols, rows, acc, zs, zr, xs, xr, ys, yr, ds, dr, ls, fs,
):
    fetches = [
        pltpu.make_async_copy(src, dst, fs.at[i])
        for i, (src, dst) in enumerate(
            (
                (k_mask_hbm, k_mask_ref),
                (k_hbm, k_ref),
                (p_mask_hbm, p_mask_ref),
                (p_hbm, p_ref),
                (atoms_hbm, atoms_ref),
                (classes_hbm, classes_ref),
                (rates_hbm, rates_ref),
            )
        )
    ]
    for copy in fetches:
        copy.start()
    r = lax.axis_index("row")
    z = lax.axis_index("col")
    d = lax.axis_index("depth")
    x = r // 2
    q = r % 2
    nx = nr // 2
    rows_here, cols_here = k_ref.shape[1], k_ref.shape[2]
    rows_out = rows_here // nd
    per_row = rows_here // cols_here
    half = nz // 2
    own_rows = pl.ds(pl.multiple_of(d * rows_out, rows_out), rows_out)

    def rx(step):
        return 2 * lax.rem(x + (step + nx), nx) + q

    def zz(step):
        return lax.rem(z + (step + nz), nz)

    up_z, down_z = (r, zz(1), d), (r, zz(-1), d)
    up_x, down_x = (rx(1), z, d), (rx(-1), z, d)
    twin = (2 * x + 1 - q, z, d)
    z_to = (up_z, down_z)
    x_to = (up_x, down_x)
    up_y, down_y = (r, z, lax.rem(d + 1, nd)), (r, z, lax.rem(d + nd - 1, nd))
    y_to = (up_y, down_y)

    barrier = pltpu.get_barrier_semaphore()
    for peer in (up_z, down_z, up_x, down_x, up_y, down_y, twin):
        pl.semaphore_signal(barrier, inc=1, device_id=peer, device_id_type=MESH)

    for copy in fetches:
        copy.wait()
    lane = lax.broadcasted_iota(jnp.int32, (1, cols_here), 1) // TILE
    for raw, mask_ref, comp in ((k_ref, k_mask_ref, 2), (p_ref, p_mask_ref, 0)):
        for i in range(rows_here // TILE):
            keep = jnp.zeros((1, cols_here), jnp.float32)
            for j in range(cols_here // TILE):
                keep = jnp.where(lane == j, mask_ref[j, i].astype(jnp.float32), keep)
            keep = keep.astype(jnp.bfloat16)
            tile = pl.ds(i * TILE, TILE)
            for c in (0, 1):
                cols[r, comp + c, tile, :] = raw[c, tile, :] * keep

    gammas = []
    for i in range(rows_out // TILE):
        atom_row = atoms_ref[(r * rows_here + d * rows_out) // TILE + i]
        gamma = jnp.zeros((1, cols_here), jnp.float32)
        for j in range(cols_here // TILE):
            atom_col = atoms_ref[z * (cols_here // TILE) + j]
            rate = rates_ref[classes_ref[atom_row, atom_col]]
            rate = jnp.where(atom_row != atom_col, rate, 0.0)
            gamma = jnp.where(lane == j, rate, gamma)
        gammas.append(gamma)
    acc[...] = jnp.zeros_like(acc)

    pl.semaphore_wait(barrier, 7)
    own = (cols.at[r, pl.ds(2, 2)], cols.at[r, pl.ds(0, 2)])

    piece = 2 * rows_out // CHUNKS

    def row_part(block, part):
        return rows.at[block, pl.ds(2 * (part % 2), 2), pl.ds(part // 2 * piece, piece)]

    def own_part(part):
        first = pl.multiple_of(d * rows_out + part // 2 * piece, piece)
        return own[part % 2].at[:, pl.ds(first, piece), :]

    def col_part(block, part):
        return cols.at[block, pl.ds(2 * (1 - part), 2)]

    def z_copy(way, dist, part):
        block = zz(1 - dist) if way == 0 else zz(dist - 1)
        src = own_part(part) if dist == 1 else row_part(block, part)
        return rcopy(
            src, row_part(block, part), zs.at[way, dist - 1, part],
            zr.at[way, dist - 1, part], z_to[way],
        )

    def z_arrival(way, dist, part):
        block = zz(-dist) if way == 0 else zz(dist)
        slot = row_part(block, part)
        return rcopy(
            slot, slot, zs.at[way, dist - 1, part], zr.at[way, dist - 1, part], z_to[way]
        )

    def comes(way, part, at):
        if part >= CHUNKS // 2:
            return way == 1
        up = part + jnp.maximum(2 - at, 0) < CHUNKS // 2
        return up if way == 0 else jnp.logical_not(up)

    def opposite(way, part, act):
        pred = comes(way, part, zz(1) if way == 0 else zz(-1))
        if pred is not False:
            pl.when(pred)(lambda: act(z_copy(way, half, part)))

    def quarter(block, turn):
        first = lax.rem(d + (turn + nd), nd) * rows_out
        return cols.at[block, :, pl.ds(pl.multiple_of(first, rows_out), rows_out), :]

    def x_turn(way, idx):
        return (0, nd // 2)[way if idx == 2 else idx]

    def x_copy(way, idx):
        step = 0 if idx < 2 else 1
        slot = quarter(rx(-step) if way == 0 else rx(step), x_turn(way, idx))
        return rcopy(slot, slot, xs.at[way, idx], xr.at[way, idx], x_to[way])

    def x_arrival(way, idx):
        step = 1 if idx < 2 else 2
        block = rx(-step) if way == 0 else rx(step)
        slot = quarter(block, x_turn(way, idx))
        return rcopy(slot, slot, xs.at[way, idx], xr.at[way, idx], x_to[way]), block

    y_blocks = (rx(-1), rx(1), rx(-2))

    def y_copy(way, j):
        slot = quarter(y_blocks[j], 0)
        return rcopy(slot, slot, ys.at[way, j], yr.at[way, j], y_to[way])

    def y_arrival(way, j):
        slot = quarter(y_blocks[j], -1 if way == 0 else 1)
        return rcopy(slot, slot, ys.at[way, j], yr.at[way, j], y_to[way])

    def to_twin(sem, block, turn):
        slot = quarter(block, turn)
        start(rcopy(slot, slot, ds.at[sem], dr.at[sem], twin))
        twins.append((sem, block, turn))

    def own_to_twin(part, block):
        slot = col_part(block, part)
        return rcopy(slot, slot, ds.at[part], dr.at[part], twin)

    sent = []
    twins = []

    def start(copy):
        copy.start()
        sent.append(copy)

    for part in range(CHUNKS):
        for way in (0, 1):
            start(z_copy(way, 1, part))
    for idx in (0, 1):
        for way in (0, 1):
            start(x_copy(way, idx))
    for part in (0, 1):
        start(own_to_twin(part, r))
    local = []
    for part in (0, 1):
        local.append(
            pltpu.make_async_copy(
                own[part].at[:, own_rows, :], rows.at[z, pl.ds(2 * part, 2)], ls.at[part]
            )
        )
    for copy in local:
        copy.start()
    for copy in local:
        copy.wait()

    def x_event(idx):
        for way in (0, 1):
            copy, block = x_arrival(way, idx)
            copy.wait_recv()
            if idx < 2 and idx == way:
                start(x_copy(way, 2))
            if x_turn(way, idx) == 0:
                j = 2 if idx == 2 else way
                for y_way in (0, 1):
                    start(y_copy(y_way, j))
            to_twin(2 + 2 * idx + way, block, x_turn(way, idx))

    def y_event(j):
        for way in (0, 1):
            y_arrival(way, j).wait_recv()
            to_twin(8 + 2 * j + way, y_blocks[j], -1 if way == 0 else 1)

    def twin_waits():
        for part in (0, 1):
            own_to_twin(part, r + 1 - 2 * q).wait_recv()
        for sem, block, turn in twins:
            slot = quarter(block + 1 - 2 * q, turn)
            rcopy(slot, slot, ds.at[sem], dr.at[sem], twin).wait_recv()

    def left_of(block, some):
        kre, kim, pre, pim = (rows[block, comp, some, :] for comp in range(4))
        return jnp.concatenate(
            (
                jnp.concatenate((kre, -kim, -pre, pim), axis=1),
                jnp.concatenate((kim, kre, -pim, -pre), axis=1),
            ),
            axis=0,
        )

    def right_of(block):
        start_row = pl.multiple_of(lax.rem(block, per_row) * cols_here, cols_here)
        right = cols[block // per_row, :, pl.ds(start_row, cols_here), :]
        return right.reshape(4 * cols_here, cols_here)

    def multiply(block):
        left = left_of(block, pl.ds(0, rows_out))
        acc[...] += jnp.dot(left, right_of(block), preferred_element_type=jnp.float32)

    def blocks(first, last):
        def step(o, carry):
            multiply(lax.rem(z + (nz + first) + o, nz))
            return carry

        lax.fori_loop(0, last + 1 - first, step, 0)

    events = {
        (2, 2): lambda: x_event(0),
        (3, 2): lambda: x_event(1),
        (4, 2): lambda: x_event(2),
        (5, 0): lambda: (y_event(0), y_event(1)),
        (6, 1): lambda: y_event(2),
        (6, 2): twin_waits,
        (6, 3): lambda: blocks(-5, -4),
        (7, 0): lambda: blocks(-3, -1),
        (7, 1): lambda: blocks(0, 2),
        (7, 2): lambda: blocks(3, 5),
    }
    for dist in range(1, half):
        for part in range(CHUNKS):
            for way in (1, 0):
                z_arrival(way, dist, part).wait_recv()
                if dist + 1 < half:
                    start(z_copy(way, dist + 1, part))
                else:
                    opposite(way, part, lambda copy: copy.start())
            events.get((dist, part), lambda: None)()
    blocks(6, 7)
    blocks(-7, -6)
    last = zz(half)
    right = right_of(last)
    for i in range(rows_out // TILE):
        tile = pl.ds(i * TILE, TILE)
        for part in (2 * i, 2 * i + 1):
            for way in (0, 1):
                pred = comes(way, part, z)
                if pred is not False:
                    pl.when(pred)(lambda: z_arrival(way, half, part).wait_recv())
        both = jnp.dot(left_of(last, tile), right, preferred_element_type=jnp.float32)
        z_re = acc[tile, :] + both[:TILE]
        z_im = acc[pl.ds(rows_out + i * TILE, TILE), :] + both[TILE:]
        p_re = rows[z, 2, tile, :].astype(jnp.float32)
        p_im = rows[z, 3, tile, :].astype(jnp.float32)
        out_ref[0, tile, :] = z_im - gammas[i] * p_re
        out_ref[1, tile, :] = -z_re - gammas[i] * p_im

    for copy in sent:
        copy.wait_send()
    for part in range(CHUNKS):
        for way in (0, 1):
            opposite(way, part, lambda copy: copy.wait_send())


def solution(mesh):
    nr, nz, nd = mesh.shape["row"], mesh.shape["col"], mesh.shape["depth"]

    def body(k_parts, p_parts, k_mask, p_mask, atoms, classes, rates):
        rows_here, cols_here = k_parts.shape[1:]
        rows_out = rows_here // nd
        half = nz // 2
        return pl.pallas_call(
            functools.partial(kernel, nr, nz, nd),
            out_shape=jax.ShapeDtypeStruct((2, rows_out, cols_here), jnp.float32),
            in_specs=[pl.BlockSpec(memory_space=pltpu.HBM)] * 7,
            out_specs=pl.BlockSpec(memory_space=pltpu.VMEM),
            scratch_shapes=[
                pltpu.VMEM(k_parts.shape, k_parts.dtype),
                pltpu.VMEM(p_parts.shape, p_parts.dtype),
                pltpu.SMEM(k_mask.T.shape, k_mask.dtype),
                pltpu.SMEM(p_mask.T.shape, p_mask.dtype),
                pltpu.SMEM(atoms.shape, atoms.dtype),
                pltpu.SMEM(classes.shape, classes.dtype),
                pltpu.SMEM(rates.shape, rates.dtype),
                pltpu.VMEM((nr, 4, rows_here, cols_here), jnp.bfloat16),
                pltpu.VMEM((nz, 4, rows_out, cols_here), jnp.bfloat16),
                pltpu.VMEM((2 * rows_out, cols_here), jnp.float32),
                pltpu.SemaphoreType.DMA((2, half, CHUNKS)),
                pltpu.SemaphoreType.DMA((2, half, CHUNKS)),
                pltpu.SemaphoreType.DMA((2, 3)),
                pltpu.SemaphoreType.DMA((2, 3)),
                pltpu.SemaphoreType.DMA((2, 3)),
                pltpu.SemaphoreType.DMA((2, 3)),
                pltpu.SemaphoreType.DMA((14,)),
                pltpu.SemaphoreType.DMA((14,)),
                pltpu.SemaphoreType.DMA((2,)),
                pltpu.SemaphoreType.DMA((7,)),
            ],
            compiler_params=pltpu.CompilerParams(
                collective_id=0, has_side_effects=True, vmem_limit_bytes=40 * 2**20
            ),
        )(*(pltpu.with_memory_space_constraint(v, pltpu.HBM) for v in (k_parts, p_parts, k_mask.T, p_mask.T, atoms, classes, rates)))

    return jax.shard_map(
        body,
        mesh=mesh,
        in_specs=(
            P(None, "row", "col"),
            P(None, "row", "col"),
            P("row", "col"),
            P("row", "col"),
            P(),
            P(),
            P(),
        ),
        out_specs=P(None, ("row", "depth"), "col"),
        check_vma=False,
    )
```

```python
import functools

import jax
import jax.numpy as jnp
from jax import lax
from jax.experimental import pallas as pl
from jax.experimental.pallas import tpu as pltpu
from jax.sharding import PartitionSpec as P

TILE = 64
CHUNKS = 4
MESH = pl.DeviceIdType.MESH


def rcopy(src, dst, send_sem, recv_sem, device):
    return pltpu.make_async_remote_copy(
        src_ref=src,
        dst_ref=dst,
        send_sem=send_sem,
        recv_sem=recv_sem,
        device_id=device,
        device_id_type=MESH,
    )


def kernel(
    nr, nz, nd,
    k_hbm, p_hbm, k_mask_hbm, p_mask_hbm, atoms_hbm, classes_hbm, rates_hbm,
    out_ref,
    k_ref, p_ref, k_mask_ref, p_mask_ref, atoms_ref, classes_ref, rates_ref,
    cols, rows, acc, zs, zr, xs, xr, ys, yr, ds, dr, ls, fs,
):
    fetches = [
        pltpu.make_async_copy(src, dst, fs.at[i])
        for i, (src, dst) in enumerate(
            (
                (k_mask_hbm, k_mask_ref),
                (k_hbm, k_ref),
                (p_mask_hbm, p_mask_ref),
                (p_hbm, p_ref),
                (atoms_hbm, atoms_ref),
                (classes_hbm, classes_ref),
                (rates_hbm, rates_ref),
            )
        )
    ]
    for copy in fetches:
        copy.start()
    r = lax.axis_index("row")
    z = lax.axis_index("col")
    d = lax.axis_index("depth")
    x = r // 2
    q = r % 2
    nx = nr // 2
    rows_here, cols_here = k_ref.shape[1], k_ref.shape[2]
    rows_out = rows_here // nd
    per_row = rows_here // cols_here
    half = nz // 2
    own_rows = pl.ds(pl.multiple_of(d * rows_out, rows_out), rows_out)

    def rx(step):
        return 2 * lax.rem(x + (step + nx), nx) + q

    def zz(step):
        return lax.rem(z + (step + nz), nz)

    up_z, down_z = (r, zz(1), d), (r, zz(-1), d)
    up_x, down_x = (rx(1), z, d), (rx(-1), z, d)
    twin = (2 * x + 1 - q, z, d)
    z_to = (up_z, down_z)
    x_to = (up_x, down_x)
    up_y, down_y = (r, z, lax.rem(d + 1, nd)), (r, z, lax.rem(d + nd - 1, nd))
    y_to = (up_y, down_y)

    barrier = pltpu.get_barrier_semaphore()
    for peer in (up_z, down_z, up_x, down_x, up_y, down_y, twin):
        pl.semaphore_signal(barrier, inc=1, device_id=peer, device_id_type=MESH)

    for copy in fetches:
        copy.wait()
    lane = lax.broadcasted_iota(jnp.int32, (1, cols_here), 1) // TILE
    for raw, mask_ref, comp in ((k_ref, k_mask_ref, 2), (p_ref, p_mask_ref, 0)):
        for i in range(rows_here // TILE):
            keep = jnp.zeros((1, cols_here), jnp.float32)
            for j in range(cols_here // TILE):
                keep = jnp.where(lane == j, mask_ref[j, i].astype(jnp.float32), keep)
            keep = keep.astype(jnp.bfloat16)
            tile = pl.ds(i * TILE, TILE)
            for c in (0, 1):
                cols[r, comp + c, tile, :] = raw[c, tile, :] * keep

    gammas = []
    for i in range(rows_out // TILE):
        atom_row = atoms_ref[(r * rows_here + d * rows_out) // TILE + i]
        gamma = jnp.zeros((1, cols_here), jnp.float32)
        for j in range(cols_here // TILE):
            atom_col = atoms_ref[z * (cols_here // TILE) + j]
            rate = rates_ref[classes_ref[atom_row, atom_col]]
            rate = jnp.where(atom_row != atom_col, rate, 0.0)
            gamma = jnp.where(lane == j, rate, gamma)
        gammas.append(gamma)
    acc[...] = jnp.zeros_like(acc)

    pl.semaphore_wait(barrier, 7)
    own = (cols.at[r, pl.ds(2, 2)], cols.at[r, pl.ds(0, 2)])

    piece = 2 * rows_out // CHUNKS

    def row_part(block, part):
        return rows.at[block, pl.ds(2 * (part % 2), 2), pl.ds(part // 2 * piece, piece)]

    def own_part(part):
        first = pl.multiple_of(d * rows_out + part // 2 * piece, piece)
        return own[part % 2].at[:, pl.ds(first, piece), :]

    def col_part(block, part):
        return cols.at[block, pl.ds(2 * (1 - part), 2)]

    def z_copy(way, dist, part):
        block = zz(1 - dist) if way == 0 else zz(dist - 1)
        src = own_part(part) if dist == 1 else row_part(block, part)
        return rcopy(
            src, row_part(block, part), zs.at[way, dist - 1, part],
            zr.at[way, dist - 1, part], z_to[way],
        )

    def z_arrival(way, dist, part):
        block = zz(-dist) if way == 0 else zz(dist)
        slot = row_part(block, part)
        return rcopy(
            slot, slot, zs.at[way, dist - 1, part], zr.at[way, dist - 1, part], z_to[way]
        )

    def comes(way, part, at):
        if part >= CHUNKS // 2:
            return way == 1
        up = part + jnp.clip(3 - at, 0, 2) < CHUNKS // 2
        return up if way == 0 else jnp.logical_not(up)

    def opposite(way, part, act):
        pred = comes(way, part, zz(1) if way == 0 else zz(-1))
        if pred is not False:
            pl.when(pred)(lambda: act(z_copy(way, half, part)))

    def quarter(block, turn):
        first = lax.rem(d + (turn + nd), nd) * rows_out
        return cols.at[block, :, pl.ds(pl.multiple_of(first, rows_out), rows_out), :]

    def x_turn(way, idx):
        return (0, nd // 2)[way if idx == 2 else idx]

    def x_copy(way, idx):
        step = 0 if idx < 2 else 1
        slot = quarter(rx(-step) if way == 0 else rx(step), x_turn(way, idx))
        return rcopy(slot, slot, xs.at[way, idx], xr.at[way, idx], x_to[way])

    def x_arrival(way, idx):
        step = 1 if idx < 2 else 2
        block = rx(-step) if way == 0 else rx(step)
        slot = quarter(block, x_turn(way, idx))
        return rcopy(slot, slot, xs.at[way, idx], xr.at[way, idx], x_to[way]), block

    y_blocks = (rx(-1), rx(1), rx(-2))

    def y_copy(way, j):
        slot = quarter(y_blocks[j], 0)
        return rcopy(slot, slot, ys.at[way, j], yr.at[way, j], y_to[way])

    def y_arrival(way, j):
        slot = quarter(y_blocks[j], -1 if way == 0 else 1)
        return rcopy(slot, slot, ys.at[way, j], yr.at[way, j], y_to[way])

    def to_twin(sem, block, turn):
        slot = quarter(block, turn)
        start(rcopy(slot, slot, ds.at[sem], dr.at[sem], twin))
        twins.append((sem, block, turn))

    def own_to_twin(part, block):
        slot = col_part(block, part)
        return rcopy(slot, slot, ds.at[part], dr.at[part], twin)

    sent = []
    twins = []

    def start(copy):
        copy.start()
        sent.append(copy)

    for part in range(CHUNKS):
        for way in (0, 1):
            start(z_copy(way, 1, part))
    for idx in (0, 1):
        for way in (0, 1):
            start(x_copy(way, idx))
    for part in (0, 1):
        start(own_to_twin(part, r))
    local = []
    for part in (0, 1):
        local.append(
            pltpu.make_async_copy(
                own[part].at[:, own_rows, :], rows.at[z, pl.ds(2 * part, 2)], ls.at[part]
            )
        )
    for copy in local:
        copy.start()
    for copy in local:
        copy.wait()

    def x_event(idx):
        for way in (0, 1):
            copy, block = x_arrival(way, idx)
            copy.wait_recv()
            if idx < 2 and idx == way:
                start(x_copy(way, 2))
            if x_turn(way, idx) == 0:
                j = 2 if idx == 2 else way
                for y_way in (0, 1):
                    start(y_copy(y_way, j))
            to_twin(2 + 2 * idx + way, block, x_turn(way, idx))

    def y_event(j):
        for way in (0, 1):
            y_arrival(way, j).wait_recv()
            to_twin(8 + 2 * j + way, y_blocks[j], -1 if way == 0 else 1)

    def twin_waits():
        for part in (0, 1):
            own_to_twin(part, r + 1 - 2 * q).wait_recv()
        for sem, block, turn in twins:
            slot = quarter(block + 1 - 2 * q, turn)
            rcopy(slot, slot, ds.at[sem], dr.at[sem], twin).wait_recv()

    def left_of(block, some):
        kre, kim, pre, pim = (rows[block, comp, some, :] for comp in range(4))
        return jnp.concatenate(
            (
                jnp.concatenate((kre, -kim, -pre, pim), axis=1),
                jnp.concatenate((kim, kre, -pim, -pre), axis=1),
            ),
            axis=0,
        )

    def right_of(block):
        start_row = pl.multiple_of(lax.rem(block, per_row) * cols_here, cols_here)
        right = cols[block // per_row, :, pl.ds(start_row, cols_here), :]
        return right.reshape(4 * cols_here, cols_here)

    def multiply(block):
        left = left_of(block, pl.ds(0, rows_out))
        acc[...] += jnp.dot(left, right_of(block), preferred_element_type=jnp.float32)

    def blocks(first, last):
        def step(o, carry):
            multiply(lax.rem(z + (nz + first) + o, nz))
            return carry

        lax.fori_loop(0, last + 1 - first, step, 0)

    events = {
        (2, 2): lambda: x_event(0),
        (3, 2): lambda: x_event(1),
        (4, 2): lambda: x_event(2),
        (5, 0): lambda: (y_event(0), y_event(1)),
        (6, 1): lambda: y_event(2),
        (6, 2): twin_waits,
        (6, 3): lambda: blocks(-5, -4),
        (7, 0): lambda: blocks(-3, -1),
        (7, 1): lambda: blocks(0, 2),
        (7, 2): lambda: blocks(3, 5),
    }
    for dist in range(1, half):
        for part in range(CHUNKS):
            for way in (1, 0):
                z_arrival(way, dist, part).wait_recv()
                if dist + 1 < half:
                    start(z_copy(way, dist + 1, part))
                else:
                    opposite(way, part, lambda copy: copy.start())
            events.get((dist, part), lambda: None)()
    blocks(6, 7)
    blocks(-7, -6)
    last = zz(half)
    right = right_of(last)
    for i in range(rows_out // TILE):
        tile = pl.ds(i * TILE, TILE)
        for part in (2 * i, 2 * i + 1):
            for way in (0, 1):
                pred = comes(way, part, z)
                if pred is not False:
                    pl.when(pred)(lambda: z_arrival(way, half, part).wait_recv())
        both = jnp.dot(left_of(last, tile), right, preferred_element_type=jnp.float32)
        z_re = acc[tile, :] + both[:TILE]
        z_im = acc[pl.ds(rows_out + i * TILE, TILE), :] + both[TILE:]
        p_re = rows[z, 2, tile, :].astype(jnp.float32)
        p_im = rows[z, 3, tile, :].astype(jnp.float32)
        out_ref[0, tile, :] = z_im - gammas[i] * p_re
        out_ref[1, tile, :] = -z_re - gammas[i] * p_im

    for copy in sent:
        copy.wait_send()
    for part in range(CHUNKS):
        for way in (0, 1):
            opposite(way, part, lambda copy: copy.wait_send())


def solution(mesh):
    nr, nz, nd = mesh.shape["row"], mesh.shape["col"], mesh.shape["depth"]

    def body(k_parts, p_parts, k_mask, p_mask, atoms, classes, rates):
        rows_here, cols_here = k_parts.shape[1:]
        rows_out = rows_here // nd
        half = nz // 2
        return pl.pallas_call(
            functools.partial(kernel, nr, nz, nd),
            out_shape=jax.ShapeDtypeStruct((2, rows_out, cols_here), jnp.float32),
            in_specs=[pl.BlockSpec(memory_space=pltpu.HBM)] * 7,
            out_specs=pl.BlockSpec(memory_space=pltpu.VMEM),
            scratch_shapes=[
                pltpu.VMEM(k_parts.shape, k_parts.dtype),
                pltpu.VMEM(p_parts.shape, p_parts.dtype),
                pltpu.SMEM(k_mask.T.shape, k_mask.dtype),
                pltpu.SMEM(p_mask.T.shape, p_mask.dtype),
                pltpu.SMEM(atoms.shape, atoms.dtype),
                pltpu.SMEM(classes.shape, classes.dtype),
                pltpu.SMEM(rates.shape, rates.dtype),
                pltpu.VMEM((nr, 4, rows_here, cols_here), jnp.bfloat16),
                pltpu.VMEM((nz, 4, rows_out, cols_here), jnp.bfloat16),
                pltpu.VMEM((2 * rows_out, cols_here), jnp.float32),
                pltpu.SemaphoreType.DMA((2, half, CHUNKS)),
                pltpu.SemaphoreType.DMA((2, half, CHUNKS)),
                pltpu.SemaphoreType.DMA((2, 3)),
                pltpu.SemaphoreType.DMA((2, 3)),
                pltpu.SemaphoreType.DMA((2, 3)),
                pltpu.SemaphoreType.DMA((2, 3)),
                pltpu.SemaphoreType.DMA((14,)),
                pltpu.SemaphoreType.DMA((14,)),
                pltpu.SemaphoreType.DMA((2,)),
                pltpu.SemaphoreType.DMA((7,)),
            ],
            compiler_params=pltpu.CompilerParams(
                collective_id=0, has_side_effects=True, vmem_limit_bytes=40 * 2**20
            ),
        )(*(pltpu.with_memory_space_constraint(v, pltpu.HBM) for v in (k_parts, p_parts, k_mask.T, p_mask.T, atoms, classes, rates)))

    return jax.shard_map(
        body,
        mesh=mesh,
        in_specs=(
            P(None, "row", "col"),
            P(None, "row", "col"),
            P("row", "col"),
            P("row", "col"),
            P(),
            P(),
            P(),
        ),
        out_specs=P(None, ("row", "depth"), "col"),
        check_vma=False,
    )
```
